512 devices in a mesh: section: 4 (over z_hi, core), ctx: 16 (over y, x), tp: 8 (over z_lo).
Axes of the slice: x: 4, y: 4, z: 16 (z_hi: 2, z_lo: 8; z = z_hi * 8 + z_lo), core: 2. Of those that a mesh axis runs over, the one named last changes fastest.
Arguments:
- query_heads: bfloat16 [8192, 8, 1024], P('ctx', 'tp', 'section'), may hold values from -10 to 10
- key_cache: bfloat16 [16, 512, 1024], P('ctx', ('section', 'tp')), may hold values from -4 to 4
- value_cache: bfloat16 [16, 512, 1024], P('ctx', ('section', 'tp')), may hold values from -6 to 6
- doc_lengths: int32 [4], replicated, may hold values from 1 to 5120, 8192 in all
Outputs:
- attended: bfloat16 [8192, 8, 1024], P('ctx', 'tp', 'section')
The draws below stay inside these ranges and needn't reach their ends.
All inputs are finite; a program needn't handle non-finite values.
Results may differ from the reference program's by a relative error of at most 0.0044.
Values may be sent and summed in bfloat16 or wider, within the bound.
No kernel may reach another device: no remote copies, remote signals or barrier semaphores. Data moves between devices by JAX's collectives and lax.ppermute only.
A program may use at most 64 MiB of HBM per device.

```python
import math
import jax
import jax.numpy as jnp
import numpy as np
from jax import lax

KVH = 8
GROUP = 8
HD = 128
BLK = 512
NDOC = 4
SEQ = 8192
N_CTX = 16


def draw_key_cache(key, part):
    table = jnp.clip(jax.random.normal(jax.random.fold_in(key, 11), (SEQ, KVH, HD), jnp.float32), -4.0, 4.0)
    return table.reshape(SEQ // BLK, BLK, KVH * HD).astype(jnp.bfloat16)


def draw_query_heads(key, part):
    table = jnp.clip(jax.random.normal(jax.random.fold_in(key, 17), (SEQ, KVH, GROUP, HD), jnp.float32), -4.0, 4.0)
    return table.reshape(SEQ, KVH, GROUP * HD).astype(jnp.bfloat16)


def block_scale(stream_key, extent, pieces, least, top_value):
    def one(dim, shards_of):
        steps = jax.random.uniform(jax.random.fold_in(jax.random.fold_in(stream_key, 6), dim), (shards_of,), jnp.float32, least / len(pieces), top_value / len(pieces))
        return jnp.repeat(jnp.exp(steps), extent[dim] // shards_of).reshape((-1,) + (1,) * (len(extent) - dim - 1))

    gain = one(*pieces[0])
    for cut in pieces[1:]:
        gain = gain * one(*cut)
    return gain


def length_profile(number_of, total, reach, lean):
    weights = [(1 << 20) // math.isqrt(rank ** lean) + 1 for rank in range(2, number_of + 1)]
    spare, given = total - reach - (number_of - 1), [1] * (number_of - 1)
    while spare > 0:
        movable = [i for i in range(number_of - 1) if given[i] < reach]
        whole, left = sum([weights[i] for i in movable]), spare
        for i in movable:
            extra = min(reach - given[i], max(1, left * weights[i] // whole), spare)
            given[i] = given[i] + extra
            spare = spare - extra
    return np.array([reach] + given)


def uneven(key, number_of, total, most, skew):
    if number_of == 2:
        one = jax.random.randint(key, (), max(1, total - most), min(most, total - 1) + 1)
        return jnp.stack([one, total - one])
    sizes = jnp.asarray(length_profile(number_of, total, most, skew), jnp.int32)
    pairs = (number_of - 1) // 2
    source_of, sink = sizes[1:1 + 2 * pairs:2], sizes[2:2 + 2 * pairs:2]
    slack = jnp.minimum(source_of - 1, most - sink)
    moved = jax.random.randint(jax.random.fold_in(key, 1), (pairs,), 0, 1 << 20) % (slack + 1)
    sizes = sizes.at[1:1 + 2 * pairs:2].set(source_of - moved).at[2:2 + 2 * pairs:2].set(sink + moved)
    return sizes[jax.random.permutation(jax.random.fold_in(key, 2), number_of)]


def noise(rng, shape, scale, reach, shards=(), held_as=jnp.bfloat16):
    values = jax.random.normal(rng, shape, jnp.float32) * scale
    if len(shards) > 0:
        values = block_scale(rng, shape, shards, -0.22, 0.18) * values
    return jnp.clip(values, min=-reach, max=reach).astype(held_as)


def setup_inputs(seed: int = 0) -> dict:
    keys = jax.random.split(jax.random.key(seed), 5)
    query_heads = draw_query_heads(jax.random.fold_in(keys[4], 71), 0)
    key_cache = draw_key_cache(jax.random.fold_in(keys[4], 71), 0)
    value_cache = noise(keys[2], (N_CTX, BLK, KVH * HD), 1.0, 6.0, ((0, 16), (1, 32)))
    doc_lengths = uneven(keys[3], NDOC, SEQ, 5 * SEQ // 8, 2).astype(jnp.int32)
    return dict(query_heads=query_heads, key_cache=key_cache, value_cache=value_cache, doc_lengths=doc_lengths)


def reference(query_heads, key_cache, value_cache, doc_lengths):
    positions = jnp.arange(SEQ, dtype=jnp.int32)
    doc_ends = jnp.cumsum(doc_lengths).astype(jnp.int32)
    segment = jnp.sum((positions[:, None] >= doc_ends[None, :]).astype(jnp.int32), axis=1)
    allowed = (positions[None, :] <= positions[:, None]) & (segment[None, :] == segment[:, None])
    key_heads = key_cache.reshape(SEQ, KVH, HD).transpose(1, 0, 2)
    value_heads = value_cache.reshape(SEQ, KVH, HD).transpose(1, 0, 2)
    query_split = query_heads.reshape(SEQ, KVH * GROUP, HD).transpose(1, 0, 2)
    scale_factor = HD ** -0.5

    def one_head(head_index):
        queries = query_split[head_index]
        keys_now = key_heads[head_index // GROUP]
        values_now = value_heads[head_index // GROUP]
        scores = jnp.dot(queries, keys_now.T, preferred_element_type=jnp.float32) * scale_factor
        masked = jnp.where(allowed, scores, -1e30)
        top_score = jnp.max(masked, axis=1, keepdims=True)
        weights = jnp.where(allowed, jnp.exp(scores - top_score), 0.0)
        total = jnp.sum(weights, axis=1, keepdims=True)
        numerator = jnp.dot(weights.astype(jnp.bfloat16), values_now, preferred_element_type=jnp.float32)
        return (numerator / total).astype(jnp.bfloat16)

    result = lax.map(one_head, jnp.arange(KVH * GROUP, dtype=jnp.int32))
    return result.transpose(1, 0, 2).reshape(SEQ, KVH, GROUP * HD)
```

```python
import math

import jax
import jax.numpy as jnp
from jax import lax
from jax.experimental import pallas as pl
from jax.experimental.pallas import tpu as pltpu
from jax.sharding import Mesh
from jax.sharding import PartitionSpec as P

HD = 128
NDOC = 4
ROWS = 512
LOW = -1e29
HIDDEN = -1e30
STEP = math.log2(math.e) / math.sqrt(HD)
HOPS = ((1, 4), (2, 8), (3, 7), (5, 6), (9, 10))


def attend_block(q_ref, blk_ref, which, block, starts, state, first_needed, last_start):
    m_ref, l_ref, acc_ref = state
    base = which * ROWS
    heads = q_ref.shape[1] // HD

    def visit(masked):
        keys = blk_ref[:, 0].reshape(ROWS, HD)
        values = blk_ref[:, 1].reshape(ROWS, HD)
        if masked:
            n = lax.broadcasted_iota(jnp.int32, (ROWS, ROWS), 0)
            row = (n & 127) + ((n >> 7) & 1) * 256 + (n >> 8) * 128 + base
            query = block * ROWS + lax.broadcasted_iota(jnp.int32, (1, ROWS), 1)
            begin = jnp.zeros_like(query)
            for s in starts:
                begin = jnp.where(query >= s, s, begin)
            allowed = (row <= query) & (row >= begin)
        for h in range(heads):
            scores = lax.dot_general(
                keys,
                q_ref[:, h * HD : (h + 1) * HD],
                (((1,), (1,)), ((), ())),
                preferred_element_type=jnp.float32,
            )
            if masked:
                scores = jnp.where(allowed, scores, HIDDEN)
            old = m_ref[h]
            new = jnp.maximum(old, jnp.max(scores, axis=0, keepdims=True))
            weights = jnp.exp2((scores - new) * STEP)
            rescale = jnp.exp2((old - new) * STEP)
            m_ref[h] = new
            l_ref[h] = l_ref[h] * rescale + jnp.sum(weights, axis=0, keepdims=True)
            acc_ref[h] = acc_ref[h] * rescale + lax.dot_general(
                values,
                weights.astype(jnp.bfloat16),
                (((0,), (0,)), ((), ())),
                preferred_element_type=jnp.float32,
            )

    needed = (which >= 0) & (base + ROWS > first_needed)
    whole = (which < block) & (base >= last_start)

    @pl.when(needed & whole)
    def _():
        visit(False)

    @pl.when(needed & jnp.logical_not(whole))
    def _():
        visit(True)


def doc_starts(lengths_ref):
    starts = []
    total = 0
    for d in range(NDOC - 1):
        total = total + lengths_ref[d]
        starts.append(total)
    return starts


def start_of(position, starts):
    begin = 0
    for s in starts:
        begin = jnp.where(position >= s, s, begin)
    return begin


def own_kernel(lengths_ref, q_ref, blk_ref, m_ref, l_ref, acc_ref):
    block = lax.axis_index("ctx")
    starts = doc_starts(lengths_ref)
    m_ref[...] = jnp.full(m_ref.shape, LOW, jnp.float32)
    l_ref[...] = jnp.zeros(l_ref.shape, jnp.float32)
    acc_ref[...] = jnp.zeros(acc_ref.shape, jnp.float32)
    attend_block(
        q_ref, blk_ref, block, block, starts, (m_ref, l_ref, acc_ref),
        start_of(block * ROWS, starts), start_of(block * ROWS + ROWS - 1, starts),
    )


def rest_kernel(hops, lengths_ref, q_ref, *refs):
    blocks = refs[: len(hops)]
    m_in, l_in, acc_in, out_ref, m_ref, l_ref, acc_ref = refs[len(hops) :]
    block = lax.axis_index("ctx")
    core = lax.axis_index("core")
    starts = doc_starts(lengths_ref)
    m_ref[...] = m_in[...]
    l_ref[...] = l_in[...]
    acc_ref[...] = acc_in[...]
    for blk_ref, (k0, k1) in zip(blocks, hops):
        attend_block(
            q_ref, blk_ref, block - jnp.where(core == 0, k0, k1), block, starts,
            (m_ref, l_ref, acc_ref),
            start_of(block * ROWS, starts), start_of(block * ROWS + ROWS - 1, starts),
        )
    for h in range(acc_ref.shape[0]):
        attended = acc_ref[h] / l_ref[h]
        out_ref[:, h * HD : (h + 1) * HD] = attended.T.astype(jnp.bfloat16)


def in_vmem(n):
    return [pl.BlockSpec(memory_space=pltpu.VMEM)] * n


def shards(query_heads, key_cache, value_cache, doc_lengths):
    rows, _, width = query_heads.shape
    queries = query_heads.reshape(rows, width)
    heads = width // HD
    part = key_cache.shape[1]
    tp = lax.axis_size("tp")
    blocks = lax.axis_size("ctx")

    def by_head(cache):
        return cache.reshape(part, tp, HD).transpose(1, 0, 2)

    send = jnp.stack((by_head(key_cache), by_head(value_cache)), axis=1)
    send = jnp.concatenate((send, send), axis=0)
    half = lax.all_to_all(send, ("zhi", "tp"), split_axis=0, concat_axis=0, tiled=True)
    own = lax.all_gather(half, "core", axis=0, tiled=True)

    arrived = []
    for k0, k1 in HOPS:
        pairs = [(b, b + k0) for b in range(blocks - k0)]
        pairs += [(blocks + b, blocks + b + k1) for b in range(blocks - k1)]
        arrived.append(lax.ppermute(own, ("core", "ctx"), pairs))
    swapped = [lax.ppermute(a, "core", [(0, 1), (1, 0)]) for a in arrived]

    state_shape = (
        jax.ShapeDtypeStruct((heads, 1, rows), jnp.float32),
        jax.ShapeDtypeStruct((heads, 1, rows), jnp.float32),
        jax.ShapeDtypeStruct((heads, HD, rows), jnp.float32),
    )
    smem = [pl.BlockSpec(memory_space=pltpu.SMEM)]
    state = pl.pallas_call(
        own_kernel,
        out_shape=state_shape,
        in_specs=smem + in_vmem(2),
        out_specs=tuple(in_vmem(3)),
        name="own_block",
    )(doc_lengths, queries, own)
    hops = list(HOPS) + [(k1, k0) for k0, k1 in HOPS]
    out = pl.pallas_call(
        lambda *refs: rest_kernel(hops, *refs),
        out_shape=jax.ShapeDtypeStruct((rows, width), jnp.bfloat16),
        in_specs=smem + in_vmem(1 + len(hops) + 3),
        out_specs=in_vmem(1)[0],
        scratch_shapes=[pltpu.VMEM(s.shape, s.dtype) for s in state_shape],
        name="earlier_blocks",
    )(doc_lengths, queries, *arrived, *swapped, *state)
    return out.reshape(query_heads.shape)


def solution(mesh):
    cut = Mesh(
        mesh.devices.reshape(2, 2, *mesh.devices.shape[1:]), ("zhi", "core", "ctx", "tp")
    )
    cache = P("ctx", ("zhi", "core", "tp"), None)
    heads = P("ctx", "tp", ("zhi", "core"))
    return jax.shard_map(
        shards, mesh=cut, in_specs=(heads, cache, cache, P()), out_specs=heads, check_vma=False
    )
```

```python
import math

import jax
import jax.numpy as jnp
from jax import lax
from jax.experimental import pallas as pl
from jax.experimental.pallas import tpu as pltpu
from jax.sharding import Mesh
from jax.sharding import PartitionSpec as P

HD = 128
NDOC = 4
ROWS = 512
LOW = -1e29
HIDDEN = -1e30
STEP = math.log2(math.e) / math.sqrt(HD)
HOPS = ((1, 4), (2, 8), (3, 7), (5, 6), (9, 10))


def attend_block(q_ref, blk_ref, which, block, starts, state, first_needed, last_start):
    m_ref, l_ref, acc_ref = state
    base = which * ROWS
    heads = q_ref.shape[1] // HD

    def visit(masked):
        keys = blk_ref[:, 0].reshape(ROWS, HD)
        values = blk_ref[:, 1].reshape(ROWS, HD)
        if masked:
            n = lax.broadcasted_iota(jnp.int32, (ROWS, ROWS), 0)
            row = (n & 127) + ((n >> 7) & 1) * 256 + (n >> 8) * 128 + base
            query = block * ROWS + lax.broadcasted_iota(jnp.int32, (1, ROWS), 1)
            begin = jnp.zeros_like(query)
            for s in starts:
                begin = jnp.where(query >= s, s, begin)
            allowed = (row <= query) & (row >= begin)
        for h in range(heads):
            scores = lax.dot_general(
                keys,
                q_ref[:, h * HD : (h + 1) * HD],
                (((1,), (1,)), ((), ())),
                preferred_element_type=jnp.float32,
            )
            if masked:
                scores = jnp.where(allowed, scores, HIDDEN)
            old = m_ref[h]
            new = jnp.maximum(old, jnp.max(scores, axis=0, keepdims=True))
            weights = jnp.exp2((scores - new) * STEP)
            rescale = jnp.exp2((old - new) * STEP)
            m_ref[h] = new
            l_ref[h] = l_ref[h] * rescale + jnp.sum(weights, axis=0, keepdims=True)
            acc_ref[h] = acc_ref[h] * rescale + lax.dot_general(
                values,
                weights.astype(jnp.bfloat16),
                (((0,), (0,)), ((), ())),
                preferred_element_type=jnp.float32,
            )

    needed = (which >= 0) & (base + ROWS > first_needed)
    whole = (which < block) & (base >= last_start)

    @pl.when(needed & whole)
    def _():
        visit(False)

    @pl.when(needed & jnp.logical_not(whole))
    def _():
        visit(True)


def doc_starts(lengths_ref):
    starts = []
    total = 0
    for d in range(NDOC - 1):
        total = total + lengths_ref[d]
        starts.append(total)
    return starts


def start_of(position, starts):
    begin = 0
    for s in starts:
        begin = jnp.where(position >= s, s, begin)
    return begin


def stage_kernel(hops, first, last, lengths_ref, q_ref, *refs):
    blocks, refs = refs[: len(hops)], refs[len(hops) :]
    before, refs = ((), refs) if first else (refs[:3], refs[3:])
    out_ref, refs = (refs[0], refs[1:]) if last else (None, refs)
    state = refs
    m_ref, l_ref, acc_ref = state
    block = lax.axis_index("ctx")
    core = lax.axis_index("core")
    starts = doc_starts(lengths_ref)
    if first:
        m_ref[...] = jnp.full(m_ref.shape, LOW, jnp.float32)
        l_ref[...] = jnp.zeros(l_ref.shape, jnp.float32)
        acc_ref[...] = jnp.zeros(acc_ref.shape, jnp.float32)
    else:
        for ref, was in zip(state, before):
            ref[...] = was[...]
    first_needed = start_of(block * ROWS, starts)
    last_start = start_of(block * ROWS + ROWS - 1, starts)
    for blk_ref, (k0, k1) in zip(blocks, hops):
        which = block - (k0 if k0 == k1 else jnp.where(core == 0, k0, k1))
        attend_block(q_ref, blk_ref, which, block, starts, state, first_needed, last_start)
    if last:
        for h in range(acc_ref.shape[0]):
            attended = acc_ref[h] / l_ref[h]
            out_ref[:, h * HD : (h + 1) * HD] = attended.T.astype(jnp.bfloat16)


def attend(lengths, queries, blocks, hops, state, last):
    rows, width = queries.shape
    heads = width // HD
    row = jax.ShapeDtypeStruct((heads, 1, rows), jnp.float32)
    state_shape = (row, row, jax.ShapeDtypeStruct((heads, HD, rows), jnp.float32))
    out_shape = jax.ShapeDtypeStruct((rows, width), jnp.bfloat16) if last else state_shape
    vmem = pl.BlockSpec(memory_space=pltpu.VMEM)
    return pl.pallas_call(
        lambda *refs: stage_kernel(hops, not state, last, *refs),
        out_shape=out_shape,
        in_specs=[pl.BlockSpec(memory_space=pltpu.SMEM)]
        + [vmem] * (1 + len(blocks) + len(state)),
        out_specs=vmem if last else (vmem,) * 3,
        scratch_shapes=[pltpu.VMEM(s.shape, s.dtype) for s in state_shape] if last else [],
        name="attend_last" if last else "attend",
    )(lengths, queries, *blocks, *state)


def shards(query_heads, key_cache, value_cache, doc_lengths):
    rows, _, width = query_heads.shape
    queries = query_heads.reshape(rows, width)
    heads = width // HD
    part = key_cache.shape[1]
    tp = lax.axis_size("tp")
    blocks = lax.axis_size("ctx")

    def by_head(cache):
        return cache.reshape(part, tp, HD).transpose(1, 0, 2)

    send = jnp.stack((by_head(key_cache), by_head(value_cache)), axis=1)
    send = jnp.concatenate((send, send), axis=0)
    half = lax.all_to_all(send, ("zhi", "tp"), split_axis=0, concat_axis=0, tiled=True)
    own = lax.all_gather(half, "core", axis=0, tiled=True)

    arrived = []
    for k0, k1 in HOPS:
        pairs = [(b, b + k0) for b in range(blocks - k0)]
        pairs += [(blocks + b, blocks + b + k1) for b in range(blocks - k1)]
        arrived.append(lax.ppermute(own, ("core", "ctx"), pairs))
    crossed = [(k1, k0) for k0, k1 in HOPS]
    swapped = []

    def swap(i, state):
        held, state = lax.optimization_barrier((arrived[i], state))
        arrived[i] = held
        swapped.append(lax.ppermute(held, "core", [(0, 1), (1, 0)]))
        return state

    def step(blocks, hops, state, last=False):
        return attend(doc_lengths, queries, blocks, hops, state, last)

    state = step([own], [(0, 0)], ())
    state = swap(0, state)
    state = swap(1, state)
    state = step(arrived[:2], HOPS[:2], state)
    state = swap(2, state)
    state = swap(3, state)
    state = step(arrived[2:4] + swapped[:2], HOPS[2:4] + tuple(crossed[:2]), state)
    state = swap(4, state)
    state = step(arrived[4:] + swapped[2:4], HOPS[4:] + tuple(crossed[2:4]), state)
    out = step(swapped[4:], crossed[4:], state, last=True)
    return out.reshape(query_heads.shape)


def solution(mesh):
    cut = Mesh(
        mesh.devices.reshape(2, 2, *mesh.devices.shape[1:]), ("zhi", "core", "ctx", "tp")
    )
    cache = P("ctx", ("zhi", "core", "tp"), None)
    heads = P("ctx", "tp", ("zhi", "core"))
    return jax.shard_map(
        shards, mesh=cut, in_specs=(heads, cache, cache, P()), out_specs=heads, check_vma=False
    )
```

```python
import math

import jax
import jax.numpy as jnp
from jax import lax
from jax.experimental import pallas as pl
from jax.experimental.pallas import tpu as pltpu
from jax.sharding import Mesh
from jax.sharding import PartitionSpec as P

HD = 128
NDOC = 4
ROWS = 512
REACH = 5120 // ROWS + 1
LOW = -1e29
HIDDEN = -1e30
STEP = math.log2(math.e) / math.sqrt(HD)


def start_of(position, starts):
    begin = jnp.zeros_like(position)
    for s in starts:
        begin = jnp.where(position >= s, s, begin)
    return begin


def attend_kernel(other, lengths_ref, q_ref, cache_ref, *refs):
    before, refs = (refs[:3], refs[3:]) if other else ((), refs)
    out_ref, refs = (refs[0], refs[1:]) if other else (None, refs)
    m_ref, l_ref, acc_ref, buf_ref, sems = refs
    keys_here = buf_ref.shape[1] * buf_ref.shape[3]
    rows, width = q_ref.shape
    heads = width // HD
    block = lax.axis_index("ctx")
    core = lax.axis_index("core")
    held_by = 1 - core if other else core
    starts = []
    total = 0
    for d in range(NDOC - 1):
        total = total + lengths_ref[d]
        starts.append(total)
    first_needed = start_of(block * rows, starts)
    last_start = start_of(block * rows + rows - 1, starts)
    lowest = jnp.maximum(first_needed // rows, block - REACH + 1)

    def fetch(j):
        return pltpu.make_async_copy(cache_ref.at[j], buf_ref.at[j], sems.at[j])

    def begin_fetch(i, carry):
        fetch(block - i).start()
        return carry

    count = block - lowest + 1
    lax.fori_loop(0, count, begin_fetch, 0)
    if other:
        for ref, was in zip((m_ref, l_ref, acc_ref), before):
            ref[...] = was[...]
    else:
        m_ref[...] = jnp.full(m_ref.shape, LOW, jnp.float32)
        l_ref[...] = jnp.zeros(l_ref.shape, jnp.float32)
        acc_ref[...] = jnp.zeros(acc_ref.shape, jnp.float32)

    def visit(j, masked):
        keys = buf_ref[j, :, 0].reshape(keys_here, HD)
        values = buf_ref[j, :, 1].reshape(keys_here, HD)
        if masked:
            n = lax.broadcasted_iota(jnp.int32, (keys_here, rows), 0)
            key = (n & 127) + (n >> 7) * 256 + held_by * 128 + j * rows
            query = block * rows + lax.broadcasted_iota(jnp.int32, (1, rows), 1)
            allowed = (key <= query) & (key >= start_of(query, starts))
        for h in range(heads):
            scores = lax.dot_general(
                keys,
                q_ref[:, h * HD : (h + 1) * HD],
                (((1,), (1,)), ((), ())),
                preferred_element_type=jnp.float32,
            )
            if masked:
                scores = jnp.where(allowed, scores, HIDDEN)
            old = m_ref[h]
            new = jnp.maximum(old, jnp.max(scores, axis=0, keepdims=True))
            weights = jnp.exp2((scores - new) * STEP)
            rescale = jnp.exp2((old - new) * STEP)
            m_ref[h] = new
            l_ref[h] = l_ref[h] * rescale + jnp.sum(weights, axis=0, keepdims=True)
            acc_ref[h] = acc_ref[h] * rescale + lax.dot_general(
                values,
                weights.astype(jnp.bfloat16),
                (((0,), (0,)), ((), ())),
                preferred_element_type=jnp.float32,
            )

    def step(i, carry):
        j = block - i
        fetch(j).wait()
        whole = (j < block) & (j * rows >= last_start)

        @pl.when(whole)
        def _():
            visit(j, False)

        @pl.when(jnp.logical_not(whole))
        def _():
            visit(j, True)

        return carry

    lax.fori_loop(0, count, step, 0)
    if other:
        for h in range(heads):
            attended = acc_ref[h] / l_ref[h]
            out_ref[:, h * HD : (h + 1) * HD] = attended.T.astype(jnp.bfloat16)


def attend(lengths, queries, cache, state):
    other = bool(state)
    rows, width = queries.shape
    heads = width // HD
    row = jax.ShapeDtypeStruct((heads, 1, rows), jnp.float32)
    state_shape = (row, row, jax.ShapeDtypeStruct((heads, HD, rows), jnp.float32))
    vmem = pl.BlockSpec(memory_space=pltpu.VMEM)
    scratch = [pltpu.VMEM(s.shape, s.dtype) for s in state_shape] if other else []
    return pl.pallas_call(
        lambda *refs: attend_kernel(other, *refs),
        out_shape=jax.ShapeDtypeStruct((rows, width), jnp.bfloat16) if other else state_shape,
        in_specs=[
            pl.BlockSpec(memory_space=pltpu.SMEM),
            vmem,
            pl.BlockSpec(memory_space=pl.ANY),
            *[vmem] * len(state),
        ],
        out_specs=vmem if other else (vmem,) * 3,
        scratch_shapes=scratch
        + [pltpu.VMEM(cache.shape, cache.dtype), pltpu.SemaphoreType.DMA((cache.shape[0],))],
        name="attend_other" if other else "attend_own",
    )(lengths, queries, cache, *state)


def shards(query_heads, key_cache, value_cache, doc_lengths):
    rows, _, width = query_heads.shape
    queries = query_heads.reshape(rows, width)
    part = key_cache.shape[1]
    tp = lax.axis_size("tp")
    blocks = lax.axis_size("ctx")

    def by_head(cache):
        return cache.reshape(part, tp, HD).transpose(1, 0, 2)

    send = jnp.stack((by_head(key_cache), by_head(value_cache)), axis=1)
    send = jnp.concatenate((send, send), axis=0)
    half = lax.all_to_all(send, ("zhi", "tp"), split_axis=0, concat_axis=0, tiled=True)
    copies = jnp.broadcast_to(half[None], (blocks, *half.shape))
    mine = lax.all_to_all(copies, "ctx", split_axis=0, concat_axis=0, tiled=True)
    theirs = lax.ppermute(mine, "core", [(0, 1), (1, 0)])
    state = attend(doc_lengths, queries, mine, ())
    out = attend(doc_lengths, queries, theirs, state)
    return out.reshape(query_heads.shape)


def solution(mesh):
    cut = Mesh(
        mesh.devices.reshape(2, 2, *mesh.devices.shape[1:]), ("zhi", "core", "ctx", "tp")
    )
    cache = P("ctx", ("zhi", "core", "tp"), None)
    heads = P("ctx", "tp", ("zhi", "core"))
    return jax.shard_map(
        shards, mesh=cut, in_specs=(heads, cache, cache, P()), out_specs=heads, check_vma=False
    )
```

```python
import math

import jax
import jax.numpy as jnp
from jax import lax
from jax.experimental import pallas as pl
from jax.experimental.pallas import tpu as pltpu
from jax.sharding import Mesh
from jax.sharding import PartitionSpec as P

HD = 128
NDOC = 4
HIDDEN = -1e30
NEVER = 1e30
ROOM = 2.0**60
STEP = math.log2(math.e) / math.sqrt(HD)
HOPS = ((1, 4), (2, 8), (3, 7), (5, 6), (9, 10))


def doc_starts(lengths_ref):
    starts = []
    total = 0
    for d in range(NDOC - 1):
        total = total + lengths_ref[d]
        starts.append(total)
    return starts


def start_of(position, starts):
    begin = jnp.zeros_like(position)
    for s in starts:
        begin = jnp.where(position >= s, s, begin)
    return begin


def key_rows(shape):
    n = lax.broadcasted_iota(jnp.int32, shape, 0)
    return (n & 127) + ((n >> 7) & 1) * 256 + (n >> 8) * 128


def stack_heads(q_ref, stacked_ref):
    rows, width = q_ref.shape
    for h in range(width // HD):
        stacked_ref[h * rows : (h + 1) * rows] = q_ref[:, h * HD : (h + 1) * HD]


def score(keys, queries):
    return lax.dot_general(
        keys, queries, (((1,), (1,)), ((), ())), preferred_element_type=jnp.float32
    )


def mix(values, weights):
    return lax.dot_general(
        values,
        weights.astype(jnp.bfloat16),
        (((0,), (0,)), ((), ())),
        preferred_element_type=jnp.float32,
    )


def fold(weights):
    n, width = weights.shape
    return jnp.sum(weights.reshape(n // 8, 8, width), axis=0)


def own_kernel(lengths_ref, q_ref, blk_ref, m_ref, l_ref, acc_ref):
    rows, width = q_ref.shape
    block = lax.axis_index("ctx")
    starts = doc_starts(lengths_ref)
    keys = blk_ref[:, 0].reshape(rows, HD)
    values = blk_ref[:, 1].reshape(rows, HD)
    key = key_rows((rows, rows)) + block * rows
    query = block * rows + lax.broadcasted_iota(jnp.int32, (1, rows), 1)
    allowed = (key <= query) & (key >= start_of(query, starts))
    for h in range(width // HD):
        at = slice(h * rows, (h + 1) * rows)
        scores = jnp.where(allowed, score(keys, q_ref[:, h * HD : (h + 1) * HD]), HIDDEN)
        top = jnp.max(scores, axis=0, keepdims=True)
        weights = jnp.exp2((scores - top) * STEP)
        m_ref[:, at] = top
        l_ref[:, at] = fold(weights)
        acc_ref[:, at] = mix(values, weights)


def earlier_kernel(lengths_ref, q_ref, m_in, l_in, acc_in, *refs):
    pieces, refs = refs[: len(HOPS)], refs[len(HOPS) :]
    out_ref, stacked_ref, m_ref, l_ref, acc_ref, buf_ref, sems = refs
    rows, width = q_ref.shape
    heads = width // HD
    block = lax.axis_index("ctx")
    starts = doc_starts(lengths_ref)
    count = block - start_of(block * rows, starts) // rows
    part = buf_ref.shape[1]

    for piece, hops in zip(pieces, HOPS):
        for c, k in enumerate(hops):

            @pl.when(k <= count)
            def _():
                pltpu.make_async_copy(
                    piece.at[c * part : (c + 1) * part], buf_ref.at[k - 1], sems.at[k - 1]
                ).start()

    stack_heads(q_ref, stacked_ref)
    l_ref[...] = l_in[...]
    acc_ref[...] = acc_in[...]
    query = block * rows + lax.broadcasted_iota(jnp.int32, (1, rows), 1)
    begin = jnp.concatenate([start_of(query, starts)] * heads, axis=1)

    def load(i):
        keys = buf_ref[i, :, 0].reshape(rows, HD)
        values = buf_ref[i, :, 1].reshape(rows, HD)
        return keys, values, (block - 1 - i) * rows

    def step(i, carry):
        pltpu.make_async_copy(pieces[0].at[0:part], buf_ref.at[i], sems.at[i]).wait()
        keys, values, base = load(i)
        cut = False
        for s in starts:
            cut = cut | ((s > base) & (s < base + rows))

        @pl.when(jnp.logical_not(cut))
        def _():
            top = jnp.where(begin <= base, m_in[...], NEVER)
            weights = jnp.exp2((score(keys, stacked_ref[...]) - top) * STEP)
            l_ref[...] += fold(weights)
            acc_ref[...] += mix(values, weights)

        @pl.when(cut)
        def _():
            key = key_rows((rows, rows)) + base
            for h in range(heads):
                at = slice(h * rows, (h + 1) * rows)
                scores = score(keys, stacked_ref[at])
                weights = jnp.exp2((scores - m_in[:, at]) * STEP)
                weights = jnp.where(key >= begin[:, at], weights, 0.0)
                l_ref[:, at] += fold(weights)
                acc_ref[:, at] += mix(values, weights)

        return carry

    lax.fori_loop(0, count, step, 0)

    fits = jnp.sum(l_ref[...], axis=0, keepdims=True) < ROOM

    @pl.when(jnp.min(fits.astype(jnp.float32)) < 0.5)
    def _():
        m_ref[...] = m_in[...]
        l_ref[...] = l_in[...]
        acc_ref[...] = acc_in[...]

        def again(i, carry):
            keys, values, base = load(i)
            key = key_rows((rows, rows)) + base
            for h in range(heads):
                at = slice(h * rows, (h + 1) * rows)
                scores = score(keys, stacked_ref[at])
                scores = jnp.where(key >= begin[:, at], scores, HIDDEN)
                old = m_ref[:, at]
                top = jnp.maximum(old, jnp.max(scores, axis=0, keepdims=True))
                weights = jnp.exp2((scores - top) * STEP)
                shrink = jnp.exp2((old - top) * STEP)
                m_ref[:, at] = top
                l_ref[:, at] = l_ref[:, at] * shrink + fold(weights)
                acc_ref[:, at] = acc_ref[:, at] * shrink + mix(values, weights)
            return carry

        lax.fori_loop(0, count, again, 0)

    total = jnp.sum(l_ref[...], axis=0, keepdims=True)
    for h in range(heads):
        at = slice(h * rows, (h + 1) * rows)
        attended = acc_ref[:, at] / total[:, at]
        out_ref[:, h * HD : (h + 1) * HD] = attended.T.astype(jnp.bfloat16)


def attend_own(lengths, queries, own):
    rows, width = queries.shape
    columns = rows * (width // HD)
    vmem = pl.BlockSpec(memory_space=pltpu.VMEM)
    return pl.pallas_call(
        own_kernel,
        out_shape=tuple(
            jax.ShapeDtypeStruct((n, columns), jnp.float32) for n in (1, 8, HD)
        ),
        in_specs=[pl.BlockSpec(memory_space=pltpu.SMEM), vmem, vmem],
        out_specs=(vmem,) * 3,
        name="attend_own",
    )(lengths, queries, own)


def attend_earlier(lengths, queries, state, pieces):
    rows, width = queries.shape
    columns = rows * (width // HD)
    shape = pieces[0].shape
    count = 2 * len(pieces)
    vmem = pl.BlockSpec(memory_space=pltpu.VMEM)
    return pl.pallas_call(
        earlier_kernel,
        out_shape=jax.ShapeDtypeStruct((rows, width), jnp.bfloat16),
        in_specs=[pl.BlockSpec(memory_space=pltpu.SMEM)]
        + [vmem] * 4
        + [pl.BlockSpec(memory_space=pl.ANY)] * len(pieces),
        out_specs=vmem,
        scratch_shapes=[pltpu.VMEM((columns, HD), jnp.bfloat16)]
        + [pltpu.VMEM((n, columns), jnp.float32) for n in (1, 8, HD)]
        + [
            pltpu.VMEM((count, shape[0] // 2, *shape[1:]), jnp.bfloat16),
            pltpu.SemaphoreType.DMA((count,)),
        ],
        name="attend_earlier",
    )(lengths, queries, *state, *pieces)


def shards(query_heads, key_cache, value_cache, doc_lengths):
    rows, _, width = query_heads.shape
    queries = query_heads.reshape(rows, width)
    part = key_cache.shape[1]
    tp = lax.axis_size("tp")
    blocks = lax.axis_size("ctx")

    def by_head(cache):
        return cache.reshape(part, tp, HD).transpose(1, 0, 2)

    send = jnp.stack((by_head(key_cache), by_head(value_cache)), axis=1)
    send = jnp.concatenate((send, send), axis=0)
    half = lax.all_to_all(send, ("zhi", "tp"), split_axis=0, concat_axis=0, tiled=True)
    own = lax.all_gather(half, "core", axis=0, tiled=True)

    arrived = []
    for k0, k1 in HOPS:
        pairs = [(b, b + k0) for b in range(blocks - k0)]
        pairs += [(blocks + b, blocks + b + k1) for b in range(blocks - k1)]
        arrived.append(lax.ppermute(own, ("core", "ctx"), pairs))
    state = attend_own(doc_lengths, queries, own)
    pieces = []
    token = state
    for a in arrived:
        a, token = lax.optimization_barrier((a, token))
        both = lax.all_gather(a, "core", axis=0, tiled=True)
        pieces.append(both)
        token = both
    out = attend_earlier(doc_lengths, queries, state, pieces)
    return out.reshape(query_heads.shape)


def solution(mesh):
    cut = Mesh(
        mesh.devices.reshape(2, 2, *mesh.devices.shape[1:]), ("zhi", "core", "ctx", "tp")
    )
    cache = P("ctx", ("zhi", "core", "tp"), None)
    heads = P("ctx", "tp", ("zhi", "core"))
    return jax.shard_map(
        shards, mesh=cut, in_specs=(heads, cache, cache, P()), out_specs=heads, check_vma=False
    )
```

```python
import math

import jax
import jax.numpy as jnp
from jax import lax
from jax.experimental import pallas as pl
from jax.experimental.pallas import tpu as pltpu
from jax.sharding import Mesh
from jax.sharding import PartitionSpec as P

HD = 128
NDOC = 4
HIDDEN = -1e30
NEVER = 1e30
ROOM = 2.0**60
STEP = math.log2(math.e) / math.sqrt(HD)
HOPS = ((1, 4), (2, 8), (3, 7), (5, 6), (9, 10))
ORDER = (0, 1, 4, 3, 2)


def doc_starts(lengths_ref):
    starts = []
    total = 0
    for d in range(NDOC - 1):
        total = total + lengths_ref[d]
        starts.append(total)
    return starts


def start_of(position, starts):
    begin = jnp.zeros_like(position)
    for s in starts:
        begin = jnp.where(position >= s, s, begin)
    return begin


def key_rows(shape):
    n = lax.broadcasted_iota(jnp.int32, shape, 0)
    return (n & 127) + ((n >> 7) & 1) * 256 + (n >> 8) * 128


def stack_heads(q_ref, stacked_ref):
    rows, width = q_ref.shape
    for h in range(width // HD):
        stacked_ref[h * rows : (h + 1) * rows] = q_ref[:, h * HD : (h + 1) * HD]


def score(keys, queries):
    return lax.dot_general(
        keys, queries, (((1,), (1,)), ((), ())), preferred_element_type=jnp.float32
    )


def mix(values, weights):
    return lax.dot_general(
        values,
        weights.astype(jnp.bfloat16),
        (((0,), (0,)), ((), ())),
        preferred_element_type=jnp.float32,
    )


def fold(weights):
    n, width = weights.shape
    return jnp.sum(weights.reshape(n // 8, 8, width), axis=0)


def own_kernel(lengths_ref, q_ref, blk_ref, m_ref, l_ref, acc_ref):
    rows, width = q_ref.shape
    block = lax.axis_index("ctx")
    starts = doc_starts(lengths_ref)
    keys = blk_ref[:, 0].reshape(rows, HD)
    values = blk_ref[:, 1].reshape(rows, HD)
    key = key_rows((rows, rows)) + block * rows
    query = block * rows + lax.broadcasted_iota(jnp.int32, (1, rows), 1)
    allowed = (key <= query) & (key >= start_of(query, starts))
    for h in range(width // HD):
        at = slice(h * rows, (h + 1) * rows)
        scores = jnp.where(allowed, score(keys, q_ref[:, h * HD : (h + 1) * HD]), HIDDEN)
        top = jnp.max(scores, axis=0, keepdims=True)
        weights = jnp.exp2((scores - top) * STEP)
        m_ref[:, at] = top
        l_ref[:, at] = fold(weights)
        acc_ref[:, at] = mix(values, weights)


def earlier_kernel(lengths_ref, q_ref, m_in, l_in, acc_in, *refs):
    pieces, refs = refs[: len(HOPS)], refs[len(HOPS) :]
    out_ref, stacked_ref, m_ref, l_ref, acc_ref, buf_ref, sems = refs
    rows, width = q_ref.shape
    heads = width // HD
    block = lax.axis_index("ctx")
    starts = doc_starts(lengths_ref)
    count = block - start_of(block * rows, starts) // rows
    part = buf_ref.shape[1]

    for piece, hops in zip(pieces, HOPS):
        for c, k in enumerate(hops):

            @pl.when(k <= count)
            def _():
                pltpu.make_async_copy(
                    piece.at[c * part : (c + 1) * part], buf_ref.at[k - 1], sems.at[k - 1]
                ).start()

    stack_heads(q_ref, stacked_ref)
    l_ref[...] = l_in[...]
    acc_ref[...] = acc_in[...]
    query = block * rows + lax.broadcasted_iota(jnp.int32, (1, rows), 1)
    begin = jnp.concatenate([start_of(query, starts)] * heads, axis=1)

    def load(i):
        keys = buf_ref[i, :, 0].reshape(rows, HD)
        values = buf_ref[i, :, 1].reshape(rows, HD)
        return keys, values, (block - 1 - i) * rows

    def step(i, carry):
        pltpu.make_async_copy(pieces[0].at[0:part], buf_ref.at[i], sems.at[i]).wait()
        keys, values, base = load(i)
        cut = False
        for s in starts:
            cut = cut | ((s > base) & (s < base + rows))

        @pl.when(jnp.logical_not(cut))
        def _():
            top = jnp.where(begin <= base, m_in[...], NEVER)
            weights = jnp.exp2((score(keys, stacked_ref[...]) - top) * STEP)
            l_ref[...] += fold(weights)
            acc_ref[...] += mix(values, weights)

        @pl.when(cut)
        def _():
            key = key_rows((rows, rows)) + base
            for h in range(heads):
                at = slice(h * rows, (h + 1) * rows)
                scores = score(keys, stacked_ref[at])
                weights = jnp.exp2((scores - m_in[:, at]) * STEP)
                weights = jnp.where(key >= begin[:, at], weights, 0.0)
                l_ref[:, at] += fold(weights)
                acc_ref[:, at] += mix(values, weights)

        return carry

    lax.fori_loop(0, count, step, 0)

    fits = jnp.sum(l_ref[...], axis=0, keepdims=True) < ROOM

    @pl.when(jnp.min(fits.astype(jnp.float32)) < 0.5)
    def _():
        m_ref[...] = m_in[...]
        l_ref[...] = l_in[...]
        acc_ref[...] = acc_in[...]

        def again(i, carry):
            keys, values, base = load(i)
            key = key_rows((rows, rows)) + base
            for h in range(heads):
                at = slice(h * rows, (h + 1) * rows)
                scores = score(keys, stacked_ref[at])
                scores = jnp.where(key >= begin[:, at], scores, HIDDEN)
                old = m_ref[:, at]
                top = jnp.maximum(old, jnp.max(scores, axis=0, keepdims=True))
                weights = jnp.exp2((scores - top) * STEP)
                shrink = jnp.exp2((old - top) * STEP)
                m_ref[:, at] = top
                l_ref[:, at] = l_ref[:, at] * shrink + fold(weights)
                acc_ref[:, at] = acc_ref[:, at] * shrink + mix(values, weights)
            return carry

        lax.fori_loop(0, count, again, 0)

    total = jnp.sum(l_ref[...], axis=0, keepdims=True)
    for h in range(heads):
        at = slice(h * rows, (h + 1) * rows)
        attended = acc_ref[:, at] / total[:, at]
        out_ref[:, h * HD : (h + 1) * HD] = attended.T.astype(jnp.bfloat16)


def attend_own(lengths, queries, own):
    rows, width = queries.shape
    columns = rows * (width // HD)
    vmem = pl.BlockSpec(memory_space=pltpu.VMEM)
    return pl.pallas_call(
        own_kernel,
        out_shape=tuple(
            jax.ShapeDtypeStruct((n, columns), jnp.float32) for n in (1, 8, HD)
        ),
        in_specs=[pl.BlockSpec(memory_space=pltpu.SMEM), vmem, vmem],
        out_specs=(vmem,) * 3,
        name="attend_own",
    )(lengths, queries, own)


def attend_earlier(lengths, queries, state, pieces):
    rows, width = queries.shape
    columns = rows * (width // HD)
    shape = pieces[0].shape
    count = 2 * len(pieces)
    vmem = pl.BlockSpec(memory_space=pltpu.VMEM)
    return pl.pallas_call(
        earlier_kernel,
        out_shape=jax.ShapeDtypeStruct((rows, width), jnp.bfloat16),
        in_specs=[pl.BlockSpec(memory_space=pltpu.SMEM)]
        + [vmem] * 4
        + [pl.BlockSpec(memory_space=pl.ANY)] * len(pieces),
        out_specs=vmem,
        scratch_shapes=[pltpu.VMEM((columns, HD), jnp.bfloat16)]
        + [pltpu.VMEM((n, columns), jnp.float32) for n in (1, 8, HD)]
        + [
            pltpu.VMEM((count, shape[0] // 2, *shape[1:]), jnp.bfloat16),
            pltpu.SemaphoreType.DMA((count,)),
        ],
        name="attend_earlier",
    )(lengths, queries, *state, *pieces)


def shards(query_heads, key_cache, value_cache, doc_lengths):
    rows, _, width = query_heads.shape
    queries = query_heads.reshape(rows, width)
    part = key_cache.shape[1]
    tp = lax.axis_size("tp")
    blocks = lax.axis_size("ctx")

    def by_head(cache):
        return cache.reshape(part, tp, HD).transpose(1, 0, 2)

    send = jnp.stack((by_head(key_cache), by_head(value_cache)), axis=1)
    send = jnp.concatenate((send, send), axis=0)
    half = lax.all_to_all(send, ("zhi", "tp"), split_axis=0, concat_axis=0, tiled=True)
    own = lax.all_gather(half, "core", axis=0, tiled=True)

    arrived = []
    for k0, k1 in HOPS:
        pairs = [(b, b + k0) for b in range(blocks - k0)]
        pairs += [(blocks + b, blocks + b + k1) for b in range(blocks - k1)]
        arrived.append(lax.ppermute(own, ("core", "ctx"), pairs))
    state = attend_own(doc_lengths, queries, own)
    pieces = list(arrived)
    token = state
    for i in ORDER:
        a, token = lax.optimization_barrier((arrived[i], token))
        pieces[i] = token = lax.all_gather(a, "core", axis=0, tiled=True)
    out = attend_earlier(doc_lengths, queries, state, pieces)
    return out.reshape(query_heads.shape)


def solution(mesh):
    cut = Mesh(
        mesh.devices.reshape(2, 2, *mesh.devices.shape[1:]), ("zhi", "core", "ctx", "tp")
    )
    cache = P("ctx", ("zhi", "core", "tp"), None)
    heads = P("ctx", "tp", ("zhi", "core"))
    return jax.shard_map(
        shards, mesh=cut, in_specs=(heads, cache, cache, P()), out_specs=heads, check_vma=False
    )
```

```python
import math

import jax
import jax.numpy as jnp
from jax import lax
from jax.experimental import pallas as pl
from jax.experimental.pallas import tpu as pltpu
from jax.sharding import Mesh
from jax.sharding import PartitionSpec as P

HD = 128
NDOC = 4
HIDDEN = -1e30
NEVER = 1e30
ROOM = 2.0**60
STEP = math.log2(math.e) / math.sqrt(HD)
HOPS = ((1, 4), (2, 8), (3, 7), (5, 6), (9, 10))
ORDER = (0, 1, 4, 3, 2)
SPLIT = 2


def doc_starts(lengths_ref):
    starts = []
    total = 0
    for d in range(NDOC - 1):
        total = total + lengths_ref[d]
        starts.append(total)
    return starts


def start_of(position, starts):
    begin = jnp.zeros_like(position)
    for s in starts:
        begin = jnp.where(position >= s, s, begin)
    return begin


def key_rows(shape):
    n = lax.broadcasted_iota(jnp.int32, shape, 0)
    return (n & 127) + ((n >> 7) & 1) * 256 + (n >> 8) * 128


def stack_heads(q_ref, stacked_ref):
    rows, width = q_ref.shape
    for h in range(width // HD):
        stacked_ref[h * rows : (h + 1) * rows] = q_ref[:, h * HD : (h + 1) * HD]


def score(keys, queries):
    return lax.dot_general(
        keys, queries, (((1,), (1,)), ((), ())), preferred_element_type=jnp.float32
    )


def mix(values, weights):
    return lax.dot_general(
        values,
        weights.astype(jnp.bfloat16),
        (((0,), (0,)), ((), ())),
        preferred_element_type=jnp.float32,
    )


def fold(weights):
    n, width = weights.shape
    return jnp.sum(weights.reshape(n // 8, 8, width), axis=0)


def own_kernel(lengths_ref, q_ref, blk_ref, m_ref, l_ref, acc_ref):
    rows, width = q_ref.shape
    block = lax.axis_index("ctx")
    starts = doc_starts(lengths_ref)
    keys = blk_ref[:, 0].reshape(rows, HD)
    values = blk_ref[:, 1].reshape(rows, HD)
    key = key_rows((rows, rows)) + block * rows
    query = block * rows + lax.broadcasted_iota(jnp.int32, (1, rows), 1)
    allowed = (key <= query) & (key >= start_of(query, starts))
    for h in range(width // HD):
        at = slice(h * rows, (h + 1) * rows)
        scores = jnp.where(allowed, score(keys, q_ref[:, h * HD : (h + 1) * HD]), HIDDEN)
        top = jnp.max(scores, axis=0, keepdims=True)
        weights = jnp.exp2((scores - top) * STEP)
        m_ref[:, at] = top
        l_ref[:, at] = fold(weights)
        acc_ref[:, at] = mix(values, weights)


def earlier_kernel(todo, last, lengths_ref, q_ref, m_in, l_in, acc_in, *refs):
    if last:
        l_own, acc_own, refs = refs[0], refs[1], refs[2:]
    pieces, refs = refs[: len(HOPS)], refs[len(HOPS) :]
    if last:
        out_ref, m_ref, l_ref, acc_ref, stacked_ref, buf_ref, sems = refs
    else:
        l_ref, acc_ref, stacked_ref, buf_ref, sems = refs
    rows, width = q_ref.shape
    heads = width // HD
    block = lax.axis_index("ctx")
    starts = doc_starts(lengths_ref)
    count = block - start_of(block * rows, starts) // rows
    part = buf_ref.shape[1]

    def fetch(slots, begin):
        for i in slots:
            for c, k in enumerate(HOPS[i]):

                @pl.when(k <= count)
                def _():
                    copy = pltpu.make_async_copy(
                        pieces[i].at[c * part : (c + 1) * part],
                        buf_ref.at[k - 1],
                        sems.at[k - 1],
                    )
                    copy.start() if begin else copy.wait()

    fetch(todo, True)
    stack_heads(q_ref, stacked_ref)
    l_ref[...] = l_in[...]
    acc_ref[...] = acc_in[...]
    query = block * rows + lax.broadcasted_iota(jnp.int32, (1, rows), 1)
    begin = jnp.concatenate([start_of(query, starts)] * heads, axis=1)
    hops = sorted(k for i in todo for k in HOPS[i])

    def load(k):
        keys = buf_ref[k - 1, :, 0].reshape(rows, HD)
        values = buf_ref[k - 1, :, 1].reshape(rows, HD)
        return keys, values, (block - k) * rows

    def step(n, carry):
        k = hops[0]
        for i, hop in enumerate(hops[1:]):
            k = jnp.where(n > i, hop, k)
        pltpu.make_async_copy(
            pieces[todo[0]].at[0:part], buf_ref.at[k - 1], sems.at[k - 1]
        ).wait()
        keys, values, base = load(k)
        cut = False
        for s in starts:
            cut = cut | ((s > base) & (s < base + rows))

        @pl.when(jnp.logical_not(cut))
        def _():
            top = jnp.where(begin <= base, m_in[...], NEVER)
            weights = jnp.exp2((score(keys, stacked_ref[...]) - top) * STEP)
            l_ref[...] += fold(weights)
            acc_ref[...] += mix(values, weights)

        @pl.when(cut)
        def _():
            key = key_rows((rows, rows)) + base
            for h in range(heads):
                at = slice(h * rows, (h + 1) * rows)
                scores = score(keys, stacked_ref[at])
                weights = jnp.exp2((scores - m_in[:, at]) * STEP)
                weights = jnp.where(key >= begin[:, at], weights, 0.0)
                l_ref[:, at] += fold(weights)
                acc_ref[:, at] += mix(values, weights)

        return carry

    here = 0
    for hop in hops:
        here = here + jnp.where(hop <= count, 1, 0)
    lax.fori_loop(0, here, step, 0)
    if not last:
        return

    fits = jnp.sum(l_ref[...], axis=0, keepdims=True) < ROOM

    @pl.when(jnp.min(fits.astype(jnp.float32)) < 0.5)
    def _():
        rest = [i for i in range(len(HOPS)) if i not in todo]
        fetch(rest, True)
        fetch(rest, False)
        m_ref[...] = m_in[...]
        l_ref[...] = l_own[...]
        acc_ref[...] = acc_own[...]

        def again(n, carry):
            keys, values, base = load(n + 1)
            key = key_rows((rows, rows)) + base
            for h in range(heads):
                at = slice(h * rows, (h + 1) * rows)
                scores = score(keys, stacked_ref[at])
                scores = jnp.where(key >= begin[:, at], scores, HIDDEN)
                old = m_ref[:, at]
                top = jnp.maximum(old, jnp.max(scores, axis=0, keepdims=True))
                weights = jnp.exp2((scores - top) * STEP)
                shrink = jnp.exp2((old - top) * STEP)
                m_ref[:, at] = top
                l_ref[:, at] = l_ref[:, at] * shrink + fold(weights)
                acc_ref[:, at] = acc_ref[:, at] * shrink + mix(values, weights)
            return carry

        lax.fori_loop(0, count, again, 0)

    total = jnp.sum(l_ref[...], axis=0, keepdims=True)
    for h in range(heads):
        at = slice(h * rows, (h + 1) * rows)
        attended = acc_ref[:, at] / total[:, at]
        out_ref[:, h * HD : (h + 1) * HD] = attended.T.astype(jnp.bfloat16)


def attend_own(lengths, queries, own):
    rows, width = queries.shape
    columns = rows * (width // HD)
    vmem = pl.BlockSpec(memory_space=pltpu.VMEM)
    return pl.pallas_call(
        own_kernel,
        out_shape=tuple(
            jax.ShapeDtypeStruct((n, columns), jnp.float32) for n in (1, 8, HD)
        ),
        in_specs=[pl.BlockSpec(memory_space=pltpu.SMEM), vmem, vmem],
        out_specs=(vmem,) * 3,
        name="attend_own",
    )(lengths, queries, own)


def attend_earlier(lengths, queries, own, state, pieces, todo, last):
    rows, width = queries.shape
    columns = rows * (width // HD)
    part, *unit = next(p for p in pieces if p is not None).shape
    count = 2 * len(pieces)
    vmem = pl.BlockSpec(memory_space=pltpu.VMEM)
    sums = [(n, columns) for n in (8, HD)]
    scratch = [pltpu.VMEM(shape, jnp.float32) for shape in [(1, columns), *sums]]
    out = jax.ShapeDtypeStruct((rows, width), jnp.bfloat16)
    given = [p for p in pieces if p is not None]
    place = [i for i, p in enumerate(pieces) if p is not None]

    def kernel(*refs):
        lead = 5 + (2 if last else 0)
        held = [None] * len(pieces)
        for i, ref in zip(place, refs[lead : lead + len(given)]):
            held[i] = ref
        earlier_kernel(todo, last, *refs[:lead], *held, *refs[lead + len(given) :])

    return pl.pallas_call(
        kernel,
        out_shape=out if last else tuple(jax.ShapeDtypeStruct(n, jnp.float32) for n in sums),
        in_specs=[pl.BlockSpec(memory_space=pltpu.SMEM)]
        + [vmem] * (4 + (2 if last else 0))
        + [pl.BlockSpec(memory_space=pl.ANY)] * len(given),
        out_specs=vmem if last else (vmem,) * 2,
        scratch_shapes=(scratch if last else [])
        + [
            pltpu.VMEM((columns, HD), jnp.bfloat16),
            pltpu.VMEM((count, part // 2, *unit), jnp.bfloat16),
            pltpu.SemaphoreType.DMA((count,)),
        ],
        name="attend_last" if last else "attend_earlier",
    )(lengths, queries, own[0], *state, *(own[1:] if last else ()), *given)


def shards(query_heads, key_cache, value_cache, doc_lengths):
    rows, _, width = query_heads.shape
    queries = query_heads.reshape(rows, width)
    part = key_cache.shape[1]
    tp = lax.axis_size("tp")
    blocks = lax.axis_size("ctx")

    def by_head(cache):
        return cache.reshape(part, tp, HD).transpose(1, 0, 2)

    send = jnp.stack((by_head(key_cache), by_head(value_cache)), axis=1)
    send = jnp.concatenate((send, send), axis=0)
    half = lax.all_to_all(send, ("zhi", "tp"), split_axis=0, concat_axis=0, tiled=True)
    own = lax.all_gather(half, "core", axis=0, tiled=True)

    arrived = []
    for k0, k1 in HOPS:
        pairs = [(b, b + k0) for b in range(blocks - k0)]
        pairs += [(blocks + b, blocks + b + k1) for b in range(blocks - k1)]
        arrived.append(lax.ppermute(own, ("core", "ctx"), pairs))
    own_state = attend_own(doc_lengths, queries, own)
    state = own_state[1:]
    pieces = [None] * len(HOPS)
    token = state
    for n, i in enumerate(ORDER):
        if n == SPLIT:
            state = attend_earlier(
                doc_lengths, queries, own_state, state, pieces, ORDER[:SPLIT], False
            )
            token = (token, state)
        a, token = lax.optimization_barrier((arrived[i], token))
        pieces[i] = token = lax.all_gather(a, "core", axis=0, tiled=True)
    out = attend_earlier(
        doc_lengths, queries, own_state, state, pieces, ORDER[SPLIT:], True
    )
    return out.reshape(query_heads.shape)


def solution(mesh):
    cut = Mesh(
        mesh.devices.reshape(2, 2, *mesh.devices.shape[1:]), ("zhi", "core", "ctx", "tp")
    )
    cache = P("ctx", ("zhi", "core", "tp"), None)
    heads = P("ctx", "tp", ("zhi", "core"))
    return jax.shard_map(
        shards, mesh=cut, in_specs=(heads, cache, cache, P()), out_specs=heads, check_vma=False
    )
```

```python
import math

import jax
import jax.numpy as jnp
from jax import lax
from jax.experimental import pallas as pl
from jax.experimental.pallas import tpu as pltpu
from jax.sharding import Mesh
from jax.sharding import PartitionSpec as P

HD = 128
NDOC = 4
HIDDEN = -1e30
NEVER = 1e30
ROOM = 2.0**60
STEP = math.log2(math.e) / math.sqrt(HD)
HOPS = ((1, 4), (2, 8), (3, 7), (5, 6), (9, 10))
ORDER = (0, 1, 4, 3, 2)
SPLIT = 2


def doc_starts(lengths_ref):
    starts = []
    total = 0
    for d in range(NDOC - 1):
        total = total + lengths_ref[d]
        starts.append(total)
    return starts


def start_of(position, starts):
    begin = jnp.zeros_like(position)
    for s in starts:
        begin = jnp.where(position >= s, s, begin)
    return begin


def key_rows(shape):
    n = lax.broadcasted_iota(jnp.int32, shape, 0)
    return (n & 127) + ((n >> 7) & 1) * 256 + (n >> 8) * 128


def stack_heads(q_ref, stacked_ref):
    rows, width = q_ref.shape
    for h in range(width // HD):
        stacked_ref[h * rows : (h + 1) * rows] = q_ref[:, h * HD : (h + 1) * HD]


def score(keys, queries):
    return lax.dot_general(
        keys, queries, (((1,), (1,)), ((), ())), preferred_element_type=jnp.float32
    )


def mix(values, weights):
    return lax.dot_general(
        values,
        weights.astype(jnp.bfloat16),
        (((0,), (0,)), ((), ())),
        preferred_element_type=jnp.float32,
    )


def fold(weights):
    n, width = weights.shape
    return jnp.sum(weights.reshape(n // 8, 8, width), axis=0)


def attend_kernel(todo, first, last, lengths_ref, q_ref, own_ref, pieces, before, out_ref, state, scratch):
    m_ref, l_ref, acc_ref = state
    stacked_ref, buf_ref, sems = scratch
    rows, width = q_ref.shape
    heads = width // HD
    block = lax.axis_index("ctx")
    starts = doc_starts(lengths_ref)
    count = block - start_of(block * rows, starts) // rows
    part = buf_ref.shape[1]

    def own_copy():
        return pltpu.make_async_copy(own_ref, buf_ref.at[0], sems.at[0])

    def fetch(slots, begin):
        for i in slots:
            for c, k in enumerate(HOPS[i]):

                @pl.when(k <= count)
                def _():
                    copy = pltpu.make_async_copy(
                        pieces[i].at[c * part : (c + 1) * part], buf_ref.at[k], sems.at[k]
                    )
                    copy.start() if begin else copy.wait()

    if first:
        own_copy().start()
    fetch(todo, True)
    stack_heads(q_ref, stacked_ref)
    query = block * rows + lax.broadcasted_iota(jnp.int32, (1, rows), 1)
    row_begin = start_of(query, starts)
    begin = jnp.concatenate([row_begin] * heads, axis=1)
    hops = sorted(k for i in todo for k in HOPS[i])

    def load(k):
        keys = buf_ref[k, :, 0].reshape(rows, HD)
        values = buf_ref[k, :, 1].reshape(rows, HD)
        return keys, values, (block - k) * rows

    def visit_own():
        keys, values, base = load(0)
        key = key_rows((rows, rows)) + base
        allowed = (key <= query) & (key >= row_begin)
        for h in range(heads):
            at = slice(h * rows, (h + 1) * rows)
            scores = jnp.where(allowed, score(keys, stacked_ref[at]), HIDDEN)
            top = jnp.max(scores, axis=0, keepdims=True)
            weights = jnp.exp2((scores - top) * STEP)
            m_ref[:, at] = top
            l_ref[:, at] = fold(weights)
            acc_ref[:, at] = mix(values, weights)

    if first:
        own_copy().wait()
        visit_own()
    else:
        for ref, was in zip(state, before):
            ref[...] = was[...]

    def step(n, carry):
        k = hops[0]
        for i, hop in enumerate(hops[1:]):
            k = jnp.where(n > i, hop, k)
        pltpu.make_async_copy(
            pieces[todo[0]].at[0:part], buf_ref.at[k], sems.at[k]
        ).wait()
        keys, values, base = load(k)
        cut = False
        for s in starts:
            cut = cut | ((s > base) & (s < base + rows))

        @pl.when(jnp.logical_not(cut))
        def _():
            top = jnp.where(begin <= base, m_ref[...], NEVER)
            weights = jnp.exp2((score(keys, stacked_ref[...]) - top) * STEP)
            l_ref[...] += fold(weights)
            acc_ref[...] += mix(values, weights)

        @pl.when(cut)
        def _():
            key = key_rows((rows, rows)) + base
            for h in range(heads):
                at = slice(h * rows, (h + 1) * rows)
                scores = score(keys, stacked_ref[at])
                weights = jnp.exp2((scores - m_ref[:, at]) * STEP)
                weights = jnp.where(key >= begin[:, at], weights, 0.0)
                l_ref[:, at] += fold(weights)
                acc_ref[:, at] += mix(values, weights)

        return carry

    here = 0
    for hop in hops:
        here = here + jnp.where(hop <= count, 1, 0)
    lax.fori_loop(0, here, step, 0)
    if not last:
        return

    fits = jnp.sum(l_ref[...], axis=0, keepdims=True) < ROOM

    @pl.when(jnp.min(fits.astype(jnp.float32)) < 0.5)
    def _():
        rest = [i for i in range(len(HOPS)) if i not in todo]
        fetch(rest, True)
        fetch(rest, False)
        if not first:
            own_copy().start()
            own_copy().wait()
        visit_own()

        def again(n, carry):
            keys, values, base = load(n + 1)
            key = key_rows((rows, rows)) + base
            for h in range(heads):
                at = slice(h * rows, (h + 1) * rows)
                scores = score(keys, stacked_ref[at])
                scores = jnp.where(key >= begin[:, at], scores, HIDDEN)
                old = m_ref[:, at]
                top = jnp.maximum(old, jnp.max(scores, axis=0, keepdims=True))
                weights = jnp.exp2((scores - top) * STEP)
                shrink = jnp.exp2((old - top) * STEP)
                m_ref[:, at] = top
                l_ref[:, at] = l_ref[:, at] * shrink + fold(weights)
                acc_ref[:, at] = acc_ref[:, at] * shrink + mix(values, weights)
            return carry

        lax.fori_loop(0, count, again, 0)

    total = jnp.sum(l_ref[...], axis=0, keepdims=True)
    for h in range(heads):
        at = slice(h * rows, (h + 1) * rows)
        attended = acc_ref[:, at] / total[:, at]
        out_ref[:, h * HD : (h + 1) * HD] = attended.T.astype(jnp.bfloat16)


def attend(lengths, queries, own, pieces, todo, state, last):
    rows, width = queries.shape
    columns = rows * (width // HD)
    vmem = pl.BlockSpec(memory_space=pltpu.VMEM)
    sums = [(n, columns) for n in (1, 8, HD)]
    out = jax.ShapeDtypeStruct((rows, width), jnp.bfloat16)
    place = [i for i, p in enumerate(pieces) if p is not None]

    def kernel(*refs):
        lead, refs = refs[:3], list(refs[3:])
        held = {i: refs.pop(0) for i in place}
        before = [refs.pop(0) for _ in state]
        out_ref = refs.pop(0) if last else None
        attend_kernel(
            todo, not state, last, *lead, held, before, out_ref, refs[:3], refs[3:]
        )

    return pl.pallas_call(
        kernel,
        out_shape=out if last else tuple(jax.ShapeDtypeStruct(n, jnp.float32) for n in sums),
        in_specs=[pl.BlockSpec(memory_space=pltpu.SMEM), vmem]
        + [pl.BlockSpec(memory_space=pl.ANY)] * (1 + len(place))
        + [vmem] * len(state),
        out_specs=vmem if last else (vmem,) * 3,
        scratch_shapes=([pltpu.VMEM(n, jnp.float32) for n in sums] if last else [])
        + [
            pltpu.VMEM((columns, HD), jnp.bfloat16),
            pltpu.VMEM((1 + 2 * len(HOPS), *own.shape), jnp.bfloat16),
            pltpu.SemaphoreType.DMA((1 + 2 * len(HOPS),)),
        ],
        name="attend_last" if last else "attend_first",
    )(lengths, queries, own, *[pieces[i] for i in place], *state)


def shards(query_heads, key_cache, value_cache, doc_lengths):
    rows, _, width = query_heads.shape
    queries = query_heads.reshape(rows, width)
    part = key_cache.shape[1]
    tp = lax.axis_size("tp")
    blocks = lax.axis_size("ctx")

    def by_head(cache):
        return cache.reshape(part, tp, HD).transpose(1, 0, 2)

    send = jnp.stack((by_head(key_cache), by_head(value_cache)), axis=1)
    send = jnp.concatenate((send, send), axis=0)
    half = lax.all_to_all(send, ("zhi", "tp"), split_axis=0, concat_axis=0, tiled=True)
    own = lax.all_gather(half, "core", axis=0, tiled=True)

    arrived = []
    for k0, k1 in HOPS:
        pairs = [(b, b + k0) for b in range(blocks - k0)]
        pairs += [(blocks + b, blocks + b + k1) for b in range(blocks - k1)]
        arrived.append(lax.ppermute(own, ("core", "ctx"), pairs))
    state = ()
    pieces = [None] * len(HOPS)
    token = own
    for n, i in enumerate(ORDER):
        if n == SPLIT:
            state = attend(doc_lengths, queries, own, pieces, ORDER[:n], (), False)
            token = (token, state)
        a, token = lax.optimization_barrier((arrived[i], token))
        pieces[i] = token = lax.all_gather(a, "core", axis=0, tiled=True)
    todo = ORDER[SPLIT:] if state else ORDER
    out = attend(doc_lengths, queries, own, pieces, todo, state, True)
    return out.reshape(query_heads.shape)


def solution(mesh):
    cut = Mesh(
        mesh.devices.reshape(2, 2, *mesh.devices.shape[1:]), ("zhi", "core", "ctx", "tp")
    )
    cache = P("ctx", ("zhi", "core", "tp"), None)
    heads = P("ctx", "tp", ("zhi", "core"))
    return jax.shard_map(
        shards, mesh=cut, in_specs=(heads, cache, cache, P()), out_specs=heads, check_vma=False
    )
```

```python
import math

import jax
import jax.numpy as jnp
from jax import lax
from jax.experimental import pallas as pl
from jax.experimental.pallas import tpu as pltpu
from jax.sharding import Mesh
from jax.sharding import PartitionSpec as P

HD = 128
NDOC = 4
HIDDEN = -1e30
NEVER = 1e30
ROOM = 2.0**60
STEP = math.log2(math.e) / math.sqrt(HD)
HOPS = ((1, 4), (2, 8), (3, 7), (5, 6), (9, 10))
ORDER = (0, 1, 4, 3, 2)
SPLIT = 2


def doc_starts(lengths_ref):
    starts = []
    total = 0
    for d in range(NDOC - 1):
        total = total + lengths_ref[d]
        starts.append(total)
    return starts


def start_of(position, starts):
    begin = jnp.zeros_like(position)
    for s in starts:
        begin = jnp.where(position >= s, s, begin)
    return begin


def key_rows(shape):
    n = lax.broadcasted_iota(jnp.int32, shape, 0)
    return (n & 127) + ((n >> 7) & 1) * 256 + (n >> 8) * 128


def score(keys, queries):
    return lax.dot_general(
        keys, queries, (((1,), (1,)), ((), ())), preferred_element_type=jnp.float32
    )


def mix(values, weights):
    return lax.dot_general(
        values,
        weights.astype(jnp.bfloat16),
        (((0,), (0,)), ((), ())),
        preferred_element_type=jnp.float32,
    )


def fold(weights):
    n, width = weights.shape
    return jnp.sum(weights.reshape(n // 8, 8, width), axis=0)


def attend_kernel(todo, first, last, lengths_ref, q_ref, own_ref, pieces, before, out_ref, state, scratch):
    m_ref, l_ref, acc_ref = state
    stacked_ref, buf_ref, sems, lead_sems = scratch
    rows, width = q_ref.shape
    heads = width // HD
    block = lax.axis_index("ctx")
    starts = doc_starts(lengths_ref)
    count = block - start_of(block * rows, starts) // rows
    part = buf_ref.shape[1]

    def own_copy():
        return pltpu.make_async_copy(own_ref, buf_ref.at[0], sems.at[0])

    def fetch(slots, begin):
        for i in slots:
            for c, k in enumerate(HOPS[i]):

                @pl.when(k <= count)
                def _():
                    copy = pltpu.make_async_copy(
                        pieces[i].at[c * part : (c + 1) * part], buf_ref.at[k], sems.at[k]
                    )
                    copy.start() if begin else copy.wait()

    lead = [
        pltpu.make_async_copy(
            q_ref.at[:, h * HD : (h + 1) * HD],
            stacked_ref.at[h * rows : (h + 1) * rows],
            lead_sems.at[h],
        )
        for h in range(heads)
    ]
    lead += [
        pltpu.make_async_copy(was, ref, lead_sems.at[heads + n])
        for n, (was, ref) in enumerate(zip(before, state))
    ]
    for copy in lead:
        copy.start()
    if first:
        own_copy().start()
    fetch(todo, True)
    query = block * rows + lax.broadcasted_iota(jnp.int32, (1, rows), 1)
    row_begin = start_of(query, starts)
    begin = jnp.concatenate([row_begin] * heads, axis=1)
    hops = sorted(k for i in todo for k in HOPS[i])

    def load(k):
        keys = buf_ref[k, :, 0].reshape(rows, HD)
        values = buf_ref[k, :, 1].reshape(rows, HD)
        return keys, values, (block - k) * rows

    def visit_own():
        keys, values, base = load(0)
        key = key_rows((rows, rows)) + base
        allowed = (key <= query) & (key >= row_begin)
        for h in range(heads):
            at = slice(h * rows, (h + 1) * rows)
            scores = jnp.where(allowed, score(keys, stacked_ref[at]), HIDDEN)
            top = jnp.max(scores, axis=0, keepdims=True)
            weights = jnp.exp2((scores - top) * STEP)
            m_ref[:, at] = top
            l_ref[:, at] = fold(weights)
            acc_ref[:, at] = mix(values, weights)

    for copy in lead:
        copy.wait()
    if first:
        own_copy().wait()
        visit_own()

    def step(n, carry):
        k = hops[0]
        for i, hop in enumerate(hops[1:]):
            k = jnp.where(n > i, hop, k)
        pltpu.make_async_copy(
            pieces[todo[0]].at[0:part], buf_ref.at[k], sems.at[k]
        ).wait()
        keys, values, base = load(k)
        cut = False
        for s in starts:
            cut = cut | ((s > base) & (s < base + rows))

        @pl.when(jnp.logical_not(cut))
        def _():
            top = jnp.where(begin <= base, m_ref[...], NEVER)
            weights = jnp.exp2((score(keys, stacked_ref[...]) - top) * STEP)
            l_ref[...] += fold(weights)
            acc_ref[...] += mix(values, weights)

        @pl.when(cut)
        def _():
            key = key_rows((rows, rows)) + base
            for h in range(heads):
                at = slice(h * rows, (h + 1) * rows)
                scores = score(keys, stacked_ref[at])
                weights = jnp.exp2((scores - m_ref[:, at]) * STEP)
                weights = jnp.where(key >= begin[:, at], weights, 0.0)
                l_ref[:, at] += fold(weights)
                acc_ref[:, at] += mix(values, weights)

        return carry

    here = 0
    for hop in hops:
        here = here + jnp.where(hop <= count, 1, 0)
    lax.fori_loop(0, here, step, 0)
    if not last:
        return

    fits = jnp.sum(l_ref[...], axis=0, keepdims=True) < ROOM

    @pl.when(jnp.min(fits.astype(jnp.float32)) < 0.5)
    def _():
        rest = [i for i in range(len(HOPS)) if i not in todo]
        fetch(rest, True)
        fetch(rest, False)
        if not first:
            own_copy().start()
            own_copy().wait()
        visit_own()

        def again(n, carry):
            keys, values, base = load(n + 1)
            key = key_rows((rows, rows)) + base
            for h in range(heads):
                at = slice(h * rows, (h + 1) * rows)
                scores = score(keys, stacked_ref[at])
                scores = jnp.where(key >= begin[:, at], scores, HIDDEN)
                old = m_ref[:, at]
                top = jnp.maximum(old, jnp.max(scores, axis=0, keepdims=True))
                weights = jnp.exp2((scores - top) * STEP)
                shrink = jnp.exp2((old - top) * STEP)
                m_ref[:, at] = top
                l_ref[:, at] = l_ref[:, at] * shrink + fold(weights)
                acc_ref[:, at] = acc_ref[:, at] * shrink + mix(values, weights)
            return carry

        lax.fori_loop(0, count, again, 0)

    total = jnp.sum(l_ref[...], axis=0, keepdims=True)
    for h in range(heads):
        at = slice(h * rows, (h + 1) * rows)
        attended = acc_ref[:, at] / total[:, at]
        out_ref[:, h * HD : (h + 1) * HD] = attended.T.astype(jnp.bfloat16)


def attend(lengths, queries, own, pieces, todo, state, last):
    rows, width = queries.shape
    columns = rows * (width // HD)
    vmem = pl.BlockSpec(memory_space=pltpu.VMEM)
    sums = [(n, columns) for n in (1, 8, HD)]
    out = jax.ShapeDtypeStruct((rows, width), jnp.bfloat16)
    place = [i for i, p in enumerate(pieces) if p is not None]

    def kernel(*refs):
        lead, refs = refs[:3], list(refs[3:])
        held = {i: refs.pop(0) for i in place}
        before = [refs.pop(0) for _ in state]
        out_ref = refs.pop(0) if last else None
        attend_kernel(
            todo, not state, last, *lead, held, before, out_ref, refs[:3], refs[3:]
        )

    return pl.pallas_call(
        kernel,
        out_shape=out if last else tuple(jax.ShapeDtypeStruct(n, jnp.float32) for n in sums),
        in_specs=[pl.BlockSpec(memory_space=pltpu.SMEM)]
        + [pl.BlockSpec(memory_space=pl.ANY)] * (2 + len(place) + len(state)),
        out_specs=vmem if last else (vmem,) * 3,
        scratch_shapes=([pltpu.VMEM(n, jnp.float32) for n in sums] if last else [])
        + [
            pltpu.VMEM((columns, HD), jnp.bfloat16),
            pltpu.VMEM((1 + 2 * len(HOPS), *own.shape), jnp.bfloat16),
            pltpu.SemaphoreType.DMA((1 + 2 * len(HOPS),)),
            pltpu.SemaphoreType.DMA((width // HD + len(sums),)),
        ],
        name="attend_last" if last else "attend_first",
    )(lengths, queries, own, *[pieces[i] for i in place], *state)


def shards(query_heads, key_cache, value_cache, doc_lengths):
    rows, _, width = query_heads.shape
    queries = query_heads.reshape(rows, width)
    part = key_cache.shape[1]
    tp = lax.axis_size("tp")
    blocks = lax.axis_size("ctx")

    def by_head(cache):
        return cache.reshape(part, tp, HD).transpose(1, 0, 2)

    send = jnp.stack((by_head(key_cache), by_head(value_cache)), axis=1)
    send = jnp.concatenate((send, send), axis=0)
    half = lax.all_to_all(send, ("zhi", "tp"), split_axis=0, concat_axis=0, tiled=True)
    own = lax.all_gather(half, "core", axis=0, tiled=True)

    arrived = []
    for k0, k1 in HOPS:
        pairs = [(b, b + k0) for b in range(blocks - k0)]
        pairs += [(blocks + b, blocks + b + k1) for b in range(blocks - k1)]
        arrived.append(lax.ppermute(own, ("core", "ctx"), pairs))
    state = ()
    pieces = [None] * len(HOPS)
    token = own
    for n, i in enumerate(ORDER):
        if n == SPLIT:
            state = attend(doc_lengths, queries, own, pieces, ORDER[:n], (), False)
            token = (token, state)
        a, token = lax.optimization_barrier((arrived[i], token))
        pieces[i] = token = lax.all_gather(a, "core", axis=0, tiled=True)
    todo = ORDER[SPLIT:] if state else ORDER
    out = attend(doc_lengths, queries, own, pieces, todo, state, True)
    return out.reshape(query_heads.shape)


def solution(mesh):
    cut = Mesh(
        mesh.devices.reshape(2, 2, *mesh.devices.shape[1:]), ("zhi", "core", "ctx", "tp")
    )
    cache = P("ctx", ("zhi", "core", "tp"), None)
    heads = P("ctx", "tp", ("zhi", "core"))
    return jax.shard_map(
        shards, mesh=cut, in_specs=(heads, cache, cache, P()), out_specs=heads, check_vma=False
    )
```

```python
import math

import jax
import jax.numpy as jnp
from jax import lax
from jax.experimental import pallas as pl
from jax.experimental.pallas import tpu as pltpu
from jax.sharding import Mesh
from jax.sharding import PartitionSpec as P

HD = 128
NDOC = 4
HIDDEN = -1e30
NEVER = 1e30
ROOM = 2.0**60
STEP = math.log2(math.e) / math.sqrt(HD)
HOPS = ((1, 4), (2, 8), (3, 7), (5, 6), (9, 10))
ORDER = (0, 1, 4, 3, 2)
SPLIT = 2


def doc_starts(lengths_ref):
    starts = []
    total = 0
    for d in range(NDOC - 1):
        total = total + lengths_ref[d]
        starts.append(total)
    return starts


def start_of(position, starts):
    begin = jnp.zeros_like(position)
    for s in starts:
        begin = jnp.where(position >= s, s, begin)
    return begin


def key_rows(shape):
    n = lax.broadcasted_iota(jnp.int32, shape, 0)
    return (n & 127) + ((n >> 7) & 1) * 256 + (n >> 8) * 128


def score(keys, queries):
    return lax.dot_general(
        keys, queries, (((1,), (1,)), ((), ())), preferred_element_type=jnp.float32
    )


def mix(values, weights):
    return lax.dot_general(
        values,
        weights.astype(jnp.bfloat16),
        (((0,), (0,)), ((), ())),
        preferred_element_type=jnp.float32,
    )


def fold(weights):
    n, width = weights.shape
    return jnp.sum(weights.reshape(n // 8, 8, width), axis=0)


def attend_kernel(todo, first, last, lengths_ref, q_ref, own_ref, pieces, before, out_ref, state, scratch):
    m_ref, l_ref, acc_ref = state
    stacked_ref, buf_ref, sems, lead_sems = scratch
    rows, width = q_ref.shape
    heads = width // HD
    block = lax.axis_index("ctx")
    starts = doc_starts(lengths_ref)
    count = block - start_of(block * rows, starts) // rows
    part = buf_ref.shape[1]

    def own_copy():
        return pltpu.make_async_copy(own_ref, buf_ref.at[0], sems.at[0])

    def fetch(slots, begin):
        for i in slots:
            for c, k in enumerate(HOPS[i]):

                @pl.when(k <= count)
                def _():
                    copy = pltpu.make_async_copy(
                        pieces[i].at[c * part : (c + 1) * part], buf_ref.at[k], sems.at[k]
                    )
                    copy.start() if begin else copy.wait()

    lead = [
        pltpu.make_async_copy(
            q_ref.at[:, h * HD : (h + 1) * HD],
            stacked_ref.at[h * rows : (h + 1) * rows],
            lead_sems.at[h],
        )
        for h in range(heads)
    ]
    lead += [
        pltpu.make_async_copy(was, ref, lead_sems.at[heads + n])
        for n, (was, ref) in enumerate(zip(before, state))
    ]
    for copy in lead:
        copy.start()
    if first:
        own_copy().start()
    fetch(todo, True)
    query = block * rows + lax.broadcasted_iota(jnp.int32, (1, rows), 1)
    row_begin = start_of(query, starts)
    begin = jnp.concatenate([row_begin] * heads, axis=1)
    hops = sorted(k for i in todo for k in HOPS[i])

    def load(k):
        keys = buf_ref[k, :, 0].reshape(rows, HD)
        values = buf_ref[k, :, 1].reshape(rows, HD)
        return keys, values, (block - k) * rows

    def visit_own():
        keys, values, base = load(0)
        key = key_rows((rows, rows)) + base
        allowed = (key <= query) & (key >= row_begin)
        for h in range(heads):
            at = slice(h * rows, (h + 1) * rows)
            scores = jnp.where(allowed, score(keys, stacked_ref[at]), HIDDEN)
            top = jnp.max(scores, axis=0, keepdims=True)
            weights = jnp.exp2((scores - top) * STEP)
            m_ref[:, at] = top
            l_ref[:, at] = fold(weights)
            acc_ref[:, at] = mix(values, weights)

    for copy in lead:
        copy.wait()
    if first:
        own_copy().wait()
        visit_own()

    def is_cut(base):
        cut = False
        for s in starts:
            cut = cut | ((s > base) & (s < base + rows))
        return cut

    for k in hops:

        @pl.when(k <= count)
        def _():
            pltpu.make_async_copy(
                pieces[todo[0]].at[0:part], buf_ref.at[k], sems.at[k]
            ).wait()

            @pl.when(jnp.logical_not(is_cut((block - k) * rows)))
            def _():
                keys, values, base = load(k)
                top = jnp.where(begin <= base, m_ref[...], NEVER)
                weights = jnp.exp2((score(keys, stacked_ref[...]) - top) * STEP)
                l_ref[...] += fold(weights)
                acc_ref[...] += mix(values, weights)

    def step(n, carry):
        k = hops[0]
        for i, hop in enumerate(hops[1:]):
            k = jnp.where(n > i, hop, k)

        @pl.when(is_cut((block - k) * rows))
        def _():
            keys, values, base = load(k)
            key = key_rows((rows, rows)) + base
            for h in range(heads):
                at = slice(h * rows, (h + 1) * rows)
                scores = score(keys, stacked_ref[at])
                weights = jnp.exp2((scores - m_ref[:, at]) * STEP)
                weights = jnp.where(key >= begin[:, at], weights, 0.0)
                l_ref[:, at] += fold(weights)
                acc_ref[:, at] += mix(values, weights)

        return carry

    here = 0
    for hop in hops:
        here = here + jnp.where(hop <= count, 1, 0)
    lax.fori_loop(0, here, step, 0)
    if not last:
        return

    fits = jnp.sum(l_ref[...], axis=0, keepdims=True) < ROOM

    @pl.when(jnp.min(fits.astype(jnp.float32)) < 0.5)
    def _():
        rest = [i for i in range(len(HOPS)) if i not in todo]
        fetch(rest, True)
        fetch(rest, False)
        if not first:
            own_copy().start()
            own_copy().wait()
        visit_own()

        def again(n, carry):
            keys, values, base = load(n + 1)
            key = key_rows((rows, rows)) + base
            for h in range(heads):
                at = slice(h * rows, (h + 1) * rows)
                scores = score(keys, stacked_ref[at])
                scores = jnp.where(key >= begin[:, at], scores, HIDDEN)
                old = m_ref[:, at]
                top = jnp.maximum(old, jnp.max(scores, axis=0, keepdims=True))
                weights = jnp.exp2((scores - top) * STEP)
                shrink = jnp.exp2((old - top) * STEP)
                m_ref[:, at] = top
                l_ref[:, at] = l_ref[:, at] * shrink + fold(weights)
                acc_ref[:, at] = acc_ref[:, at] * shrink + mix(values, weights)
            return carry

        lax.fori_loop(0, count, again, 0)

    total = jnp.sum(l_ref[...], axis=0, keepdims=True)
    for h in range(heads):
        at = slice(h * rows, (h + 1) * rows)
        attended = acc_ref[:, at] / total[:, at]
        out_ref[:, h * HD : (h + 1) * HD] = attended.T.astype(jnp.bfloat16)


def attend(lengths, queries, own, pieces, todo, state, last):
    rows, width = queries.shape
    columns = rows * (width // HD)
    vmem = pl.BlockSpec(memory_space=pltpu.VMEM)
    sums = [(n, columns) for n in (1, 8, HD)]
    out = jax.ShapeDtypeStruct((rows, width), jnp.bfloat16)
    place = [i for i, p in enumerate(pieces) if p is not None]

    def kernel(*refs):
        lead, refs = refs[:3], list(refs[3:])
        held = {i: refs.pop(0) for i in place}
        before = [refs.pop(0) for _ in state]
        out_ref = refs.pop(0) if last else None
        attend_kernel(
            todo, not state, last, *lead, held, before, out_ref, refs[:3], refs[3:]
        )

    return pl.pallas_call(
        kernel,
        out_shape=out if last else tuple(jax.ShapeDtypeStruct(n, jnp.float32) for n in sums),
        in_specs=[pl.BlockSpec(memory_space=pltpu.SMEM)]
        + [pl.BlockSpec(memory_space=pl.ANY)] * (2 + len(place) + len(state)),
        out_specs=vmem if last else (vmem,) * 3,
        scratch_shapes=([pltpu.VMEM(n, jnp.float32) for n in sums] if last else [])
        + [
            pltpu.VMEM((columns, HD), jnp.bfloat16),
            pltpu.VMEM((1 + 2 * len(HOPS), *own.shape), jnp.bfloat16),
            pltpu.SemaphoreType.DMA((1 + 2 * len(HOPS),)),
            pltpu.SemaphoreType.DMA((width // HD + len(sums),)),
        ],
        name="attend_last" if last else "attend_first",
    )(lengths, queries, own, *[pieces[i] for i in place], *state)


def shards(query_heads, key_cache, value_cache, doc_lengths):
    rows, _, width = query_heads.shape
    queries = query_heads.reshape(rows, width)
    part = key_cache.shape[1]
    tp = lax.axis_size("tp")
    blocks = lax.axis_size("ctx")

    def by_head(cache):
        return cache.reshape(part, tp, HD).transpose(1, 0, 2)

    send = jnp.stack((by_head(key_cache), by_head(value_cache)), axis=1)
    send = jnp.concatenate((send, send), axis=0)
    half = lax.all_to_all(send, ("zhi", "tp"), split_axis=0, concat_axis=0, tiled=True)
    own = lax.all_gather(half, "core", axis=0, tiled=True)

    arrived = []
    for k0, k1 in HOPS:
        pairs = [(b, b + k0) for b in range(blocks - k0)]
        pairs += [(blocks + b, blocks + b + k1) for b in range(blocks - k1)]
        arrived.append(lax.ppermute(own, ("core", "ctx"), pairs))
    state = ()
    pieces = [None] * len(HOPS)
    token = own
    for n, i in enumerate(ORDER):
        if n == SPLIT:
            state = attend(doc_lengths, queries, own, pieces, ORDER[:n], (), False)
            token = (token, state)
        a, token = lax.optimization_barrier((arrived[i], token))
        pieces[i] = token = lax.all_gather(a, "core", axis=0, tiled=True)
    todo = ORDER[SPLIT:] if state else ORDER
    out = attend(doc_lengths, queries, own, pieces, todo, state, True)
    return out.reshape(query_heads.shape)


def solution(mesh):
    cut = Mesh(
        mesh.devices.reshape(2, 2, *mesh.devices.shape[1:]), ("zhi", "core", "ctx", "tp")
    )
    cache = P("ctx", ("zhi", "core", "tp"), None)
    heads = P("ctx", "tp", ("zhi", "core"))
    return jax.shard_map(
        shards, mesh=cut, in_specs=(heads, cache, cache, P()), out_specs=heads, check_vma=False
    )
```

```python
import math

import jax
import jax.numpy as jnp
from jax import lax
from jax.experimental import pallas as pl
from jax.experimental.pallas import tpu as pltpu
from jax.sharding import Mesh
from jax.sharding import PartitionSpec as P

HD = 128
NDOC = 4
HIDDEN = -1e30
NEVER = 1e30
ROOM = 2.0**60
STEP = math.log2(math.e) / math.sqrt(HD)
HOPS = ((1, 4), (2, 8), (3, 7), (5, 6), (9, 10))
ORDER = (0, 1, 4, 3, 2)
SPLIT = 2


def doc_starts(lengths_ref):
    starts = []
    total = 0
    for d in range(NDOC - 1):
        total = total + lengths_ref[d]
        starts.append(total)
    return starts


def start_of(position, starts):
    begin = jnp.zeros_like(position)
    for s in starts:
        begin = jnp.where(position >= s, s, begin)
    return begin


def key_rows(shape):
    n = lax.broadcasted_iota(jnp.int32, shape, 0)
    return (n & 127) + ((n >> 7) & 1) * 256 + (n >> 8) * 128


def score(keys, queries):
    return lax.dot_general(
        keys, queries, (((1,), (1,)), ((), ())), preferred_element_type=jnp.float32
    )


def mix(values, weights):
    return lax.dot_general(
        values,
        weights.astype(jnp.bfloat16),
        (((0,), (0,)), ((), ())),
        preferred_element_type=jnp.float32,
    )


def fold(weights):
    n, width = weights.shape
    return jnp.sum(weights.reshape(n // 8, 8, width), axis=0)


def attend_kernel(todo, first, last, lengths_ref, q_ref, own_ref, pieces, before, out_ref, state, scratch):
    m_ref, l_ref, acc_ref = state
    stacked_ref, buf_ref, sems, lead_sems = scratch
    rows, width = q_ref.shape
    heads = width // HD
    block = lax.axis_index("ctx")
    starts = doc_starts(lengths_ref)
    count = block - start_of(block * rows, starts) // rows
    part = buf_ref.shape[1]

    def own_copy():
        return pltpu.make_async_copy(own_ref, buf_ref.at[0], sems.at[0])

    def fetch(slots, begin):
        for i in slots:
            for c, k in enumerate(HOPS[i]):

                @pl.when(k <= count)
                def _():
                    copy = pltpu.make_async_copy(
                        pieces[i].at[c * part : (c + 1) * part], buf_ref.at[k], sems.at[k]
                    )
                    copy.start() if begin else copy.wait()

    lead = [
        pltpu.make_async_copy(
            q_ref.at[:, h * HD : (h + 1) * HD],
            stacked_ref.at[h * rows : (h + 1) * rows],
            lead_sems.at[h],
        )
        for h in range(heads)
    ]
    lead += [
        pltpu.make_async_copy(was, ref, lead_sems.at[heads + n])
        for n, (was, ref) in enumerate(zip(before, state))
    ]
    for copy in lead:
        copy.start()
    if first:
        own_copy().start()
    fetch(todo, True)
    query = block * rows + lax.broadcasted_iota(jnp.int32, (1, rows), 1)
    row_begin = start_of(query, starts)
    begin = jnp.concatenate([row_begin] * heads, axis=1)
    hops = sorted(k for i in todo for k in HOPS[i])

    def load(k):
        keys = buf_ref[k, :, 0].reshape(rows, HD)
        values = buf_ref[k, :, 1].reshape(rows, HD)
        return keys, values, (block - k) * rows

    def visit_own():
        keys, values, base = load(0)
        key = key_rows((rows, rows)) + base
        allowed = (key <= query) & (key >= row_begin)
        for h in range(heads):
            at = slice(h * rows, (h + 1) * rows)
            scores = jnp.where(allowed, score(keys, stacked_ref[at]), HIDDEN)
            top = jnp.max(scores, axis=0, keepdims=True)
            weights = jnp.exp2((scores - top) * STEP)
            m_ref[:, at] = top
            l_ref[:, at] = fold(weights)
            acc_ref[:, at] = mix(values, weights)

    for copy in lead:
        copy.wait()
    if first:
        own_copy().wait()
        visit_own()

    def is_cut(base):
        cut = False
        for s in starts:
            cut = cut | ((s > base) & (s < base + rows))
        return cut

    for k in hops:

        @pl.when(k <= count)
        def _():
            pltpu.make_async_copy(
                pieces[todo[0]].at[0:part], buf_ref.at[k], sems.at[k]
            ).wait()

            @pl.when(jnp.logical_not(is_cut((block - k) * rows)))
            def _():
                keys, values, base = load(k)
                top = jnp.where(begin <= base, m_ref[...], NEVER)
                weights = jnp.exp2((score(keys, stacked_ref[...]) - top) * STEP)
                l_ref[...] += fold(weights)
                acc_ref[...] += mix(values, weights)

    def step(n, carry):
        k = hops[0]
        for i, hop in enumerate(hops[1:]):
            k = jnp.where(n > i, hop, k)

        @pl.when(is_cut((block - k) * rows))
        def _():
            keys, values, base = load(k)
            key = key_rows((rows, rows)) + base
            for h in range(heads):
                at = slice(h * rows, (h + 1) * rows)
                scores = score(keys, stacked_ref[at])
                weights = jnp.exp2((scores - m_ref[:, at]) * STEP)
                weights = jnp.where(key >= begin[:, at], weights, 0.0)
                l_ref[:, at] += fold(weights)
                acc_ref[:, at] += mix(values, weights)

        return carry

    here = 0
    for hop in hops:
        here = here + jnp.where(hop <= count, 1, 0)
    lax.fori_loop(0, here, step, 0)
    if not last:
        return

    fits = jnp.sum(l_ref[...], axis=0, keepdims=True) < ROOM

    @pl.when(jnp.min(fits.astype(jnp.float32)) < 0.5)
    def _():
        rest = [i for i in range(len(HOPS)) if i not in todo]
        fetch(rest, True)
        fetch(rest, False)
        if not first:
            own_copy().start()
            own_copy().wait()
        visit_own()

        def again(n, carry):
            keys, values, base = load(n + 1)
            key = key_rows((rows, rows)) + base
            for h in range(heads):
                at = slice(h * rows, (h + 1) * rows)
                scores = score(keys, stacked_ref[at])
                scores = jnp.where(key >= begin[:, at], scores, HIDDEN)
                old = m_ref[:, at]
                top = jnp.maximum(old, jnp.max(scores, axis=0, keepdims=True))
                weights = jnp.exp2((scores - top) * STEP)
                shrink = jnp.exp2((old - top) * STEP)
                m_ref[:, at] = top
                l_ref[:, at] = l_ref[:, at] * shrink + fold(weights)
                acc_ref[:, at] = acc_ref[:, at] * shrink + mix(values, weights)
            return carry

        lax.fori_loop(0, count, again, 0)

    share = 1.0 / jnp.sum(l_ref[...], axis=0, keepdims=True)
    for h in range(heads):
        at = slice(h * rows, (h + 1) * rows)
        attended = acc_ref[:, at] * share[:, at]
        out_ref[:, h * HD : (h + 1) * HD] = attended.T.astype(jnp.bfloat16)


def attend(lengths, queries, own, pieces, todo, state, last):
    rows, width = queries.shape
    columns = rows * (width // HD)
    vmem = pl.BlockSpec(memory_space=pltpu.VMEM)
    sums = [(n, columns) for n in (1, 8, HD)]
    out = jax.ShapeDtypeStruct((rows, width), jnp.bfloat16)
    place = [i for i, p in enumerate(pieces) if p is not None]

    def kernel(*refs):
        lead, refs = refs[:3], list(refs[3:])
        held = {i: refs.pop(0) for i in place}
        before = [refs.pop(0) for _ in state]
        out_ref = refs.pop(0) if last else None
        attend_kernel(
            todo, not state, last, *lead, held, before, out_ref, refs[:3], refs[3:]
        )

    return pl.pallas_call(
        kernel,
        out_shape=out if last else tuple(jax.ShapeDtypeStruct(n, jnp.float32) for n in sums),
        in_specs=[pl.BlockSpec(memory_space=pltpu.SMEM)]
        + [pl.BlockSpec(memory_space=pl.ANY)] * (2 + len(place) + len(state)),
        out_specs=vmem if last else (vmem,) * 3,
        scratch_shapes=([pltpu.VMEM(n, jnp.float32) for n in sums] if last else [])
        + [
            pltpu.VMEM((columns, HD), jnp.bfloat16),
            pltpu.VMEM((1 + 2 * len(HOPS), *own.shape), jnp.bfloat16),
            pltpu.SemaphoreType.DMA((1 + 2 * len(HOPS),)),
            pltpu.SemaphoreType.DMA((width // HD + len(sums),)),
        ],
        name="attend_last" if last else "attend_first",
    )(lengths, queries, own, *[pieces[i] for i in place], *state)


def shards(query_heads, key_cache, value_cache, doc_lengths):
    rows, _, width = query_heads.shape
    queries = query_heads.reshape(rows, width)
    part = key_cache.shape[1]
    tp = lax.axis_size("tp")
    blocks = lax.axis_size("ctx")

    def by_head(cache):
        return cache.reshape(part, tp, HD).transpose(1, 0, 2)

    send = jnp.stack((by_head(key_cache), by_head(value_cache)), axis=1)
    send = jnp.concatenate((send, send), axis=0)
    half = lax.all_to_all(send, ("zhi", "tp"), split_axis=0, concat_axis=0, tiled=True)
    own = lax.all_gather(half, "core", axis=0, tiled=True)

    arrived = []
    for k0, k1 in HOPS:
        pairs = [(b, b + k0) for b in range(blocks - k0)]
        pairs += [(blocks + b, blocks + b + k1) for b in range(blocks - k1)]
        arrived.append(lax.ppermute(own, ("core", "ctx"), pairs))
    state = ()
    pieces = [None] * len(HOPS)
    token = own
    for n, i in enumerate(ORDER):
        if n == SPLIT:
            state = attend(doc_lengths, queries, own, pieces, ORDER[:n], (), False)
            token = (token, state)
        a, token = lax.optimization_barrier((arrived[i], token))
        pieces[i] = token = lax.all_gather(a, "core", axis=0, tiled=True)
    todo = ORDER[SPLIT:] if state else ORDER
    out = attend(doc_lengths, queries, own, pieces, todo, state, True)
    return out.reshape(query_heads.shape)


def solution(mesh):
    cut = Mesh(
        mesh.devices.reshape(2, 2, *mesh.devices.shape[1:]), ("zhi", "core", "ctx", "tp")
    )
    cache = P("ctx", ("zhi", "core", "tp"), None)
    heads = P("ctx", "tp", ("zhi", "core"))
    return jax.shard_map(
        shards, mesh=cut, in_specs=(heads, cache, cache, P()), out_specs=heads, check_vma=False
    )
```
